32 devices in a mesh: expert: 4 (over z), dp: 8 (over y, x, core).
Axes of the slice: x: 2, y: 2, z: 4, core: 2. Of those that a mesh axis runs over, the one named last changes fastest.
Arguments:
- row_acts: bfloat16 [4, 8192, 2048], P('expert', 'dp'), may hold values from -6 to 6
- row_grads: bfloat16 [4, 8192, 768], P('expert', 'dp'), may hold values from -6 to 6
- grad_factor: bfloat16 [4, 768, 768], P('expert', None, 'dp'), may hold values from -0.21875 to 0.21875
- value_factor: bfloat16 [4, 2048, 768], P('expert', None, 'dp'), may hold values from -0.125 to 0.125
- counts: int32 [4, 8], P('expert', 'dp'), may hold values from 128 to 1024, as said below
- row_token: int32 [4, 8192], P('expert', 'dp'), may hold values from 0 to 1023, as said below
Outputs:
- influence: float32 [8192, 24], P(('expert', 'dp'))
The draws below stay inside these ranges and needn't reach their ends.
Inputs may be any that keep to these rules, and one draw needn't show every extreme that they name: counts[e, b] slots at the start of each block of 1024 slots are live; some block has all 1024 live. `row_token`: within one block of 1024 slots of one expert the ids are distinct, dead slots included.
All inputs are finite; a program needn't handle non-finite values.
Results may differ from the reference program's by a relative error of at most 0.0003.
Values may be sent and summed in bfloat16 or wider, within the bound.
A program may use at most 64 MiB of HBM per device.

```python
import jax
import jax.numpy as jnp
from jax import lax

MODEL = 2048
MOE_FF = 768
RANK = 32
QUERIES = 24
CAP = 1024
TOK_DEV = 256
EXPERTS = 4
ROWS = 8192
TOKENS = 8192


def draw_counts(key, part):
    nblocks = ROWS // CAP
    level_key = jax.random.fold_in(key, 11)
    jitter_key = jax.random.fold_in(key, 12)
    row_key = jax.random.fold_in(key, 13)
    column_key = jax.random.fold_in(key, 14)
    level = jax.random.randint(level_key, (EXPERTS, 1), CAP // 8, CAP + 1)
    jitter = jax.random.randint(jitter_key, (EXPERTS, nblocks), 0, CAP // 4 + 1)
    filled = jnp.minimum(level + jitter, CAP)
    chosen_row = jax.random.randint(row_key, (), 0, EXPERTS)
    chosen_column = jax.random.randint(column_key, (), 0, nblocks)
    row_grid = jnp.arange(EXPERTS, dtype=jnp.int32)[:, None]
    column_grid = jnp.arange(nblocks, dtype=jnp.int32)[None, :]
    marked = (row_grid == chosen_row) & (column_grid == chosen_column)
    return jnp.where(marked, CAP, filled).astype(jnp.int32)


def draw_row_token(key, part):
    nblocks = ROWS // CAP
    shard_tokens = TOK_DEV * EXPERTS
    block_keys = jax.random.split(jax.random.fold_in(key, 21), EXPERTS * nblocks)

    def one_block(block_key):
        return jax.random.permutation(block_key, shard_tokens)[:CAP]
    owner_ids = jax.vmap(one_block)(block_keys)
    return owner_ids.reshape(EXPERTS, ROWS).astype(jnp.int32)


def shard_levels(stream_key, dims, pieces, low, high):
    level, own = 1.0, jax.random.fold_in(stream_key, 6)
    for position, parts in pieces:
        draws = jnp.exp(jax.random.uniform(jax.random.fold_in(own, position), (parts,), jnp.float32, low / len(pieces), high / len(pieces)))
        level = level * jnp.repeat(draws, dims[position] // parts).reshape([-1 if axis == position else 1 for axis in range(len(dims))])
    return level


def normal_values(key, shape, spread, limit, pieces=(), kind=jnp.bfloat16):
    values = jax.random.normal(key, shape, jnp.float32) * spread
    if len(pieces) > 0:
        values = shard_levels(key, shape, pieces, -0.22, 0.18) * values
    return jnp.clip(values, min=-limit, max=limit).astype(kind)


def setup_inputs(seed: int = 0) -> dict:
    seeds = jax.random.split(jax.random.key(seed), 7)
    row_acts = normal_values(seeds[0], (EXPERTS, ROWS, MODEL), 1.0, 6.0, ((0, 4), (1, 8)))
    row_grads = normal_values(seeds[1], (EXPERTS, ROWS, MOE_FF), 1.0, 6.0, ((0, 4), (1, 8)))
    grad_factor = normal_values(seeds[2], (EXPERTS, MOE_FF, QUERIES * RANK), MOE_FF ** -0.5, 0.21875, ((0, 4), (2, 8)))
    value_factor = normal_values(seeds[3], (EXPERTS, MODEL, QUERIES * RANK), MODEL ** -0.5, 0.125, ((0, 4), (2, 8)))
    counts = draw_counts(jax.random.fold_in(seeds[6], 71), 0)
    row_token = draw_row_token(jax.random.fold_in(seeds[6], 71), 0)
    return dict(row_acts=row_acts, row_grads=row_grads, grad_factor=grad_factor, value_factor=value_factor, counts=counts, row_token=row_token)


epsilon = 1e-06

def reference(row_acts, row_grads, grad_factor, value_factor, counts, row_token):
    nblocks = ROWS // CAP
    shard_tokens = TOK_DEV * EXPERTS
    column_ids = jnp.arange(QUERIES * RANK, dtype=jnp.int32)[:, None] // RANK
    query_ids = jnp.arange(QUERIES, dtype=jnp.int32)[None, :]
    grouping = (column_ids == query_ids).astype(jnp.float32)
    slot_ids = jnp.arange(CAP, dtype=jnp.int32)

    def one_block(block_id):

        def one_expert(carry, expert_id):
            total_now, norm_now = carry
            start = (block_id * CAP).astype(jnp.int32)
            activ = lax.dynamic_slice(row_acts, (expert_id, start, jnp.int32(0)), (1, CAP, MODEL))[0]
            gradient = lax.dynamic_slice(row_grads, (expert_id, start, jnp.int32(0)), (1, CAP, MOE_FF))[0]
            acts_proj = jnp.dot(activ, value_factor[expert_id], preferred_element_type=jnp.float32)
            grads_proj = jnp.dot(gradient, grad_factor[expert_id], preferred_element_type=jnp.float32)
            scores = jnp.dot(acts_proj * grads_proj, grouping, precision=lax.Precision.HIGHEST)
            live = (slot_ids < counts[expert_id, block_id]).astype(jnp.float32)
            norms = lax.optimization_barrier(jnp.sum(jnp.square(activ.astype(jnp.float32)), 1)) * lax.optimization_barrier(jnp.sum(jnp.square(gradient.astype(jnp.float32)), 1))
            owner_ids = lax.dynamic_slice(row_token, (expert_id, start), (1, CAP))[0]
            total_now = total_now.at[owner_ids].add(scores * live[:, None])
            norm_now = norm_now.at[owner_ids].add(norms * live)
            return ((total_now, norm_now), None)
        start_carry = (jnp.zeros((shard_tokens, QUERIES), jnp.float32), jnp.zeros((shard_tokens,), jnp.float32))
        (total_now, norm_now), _ = lax.scan(one_expert, start_carry, jnp.arange(EXPERTS, dtype=jnp.int32))
        return (total_now, norm_now)
    totals, norm_sum = lax.map(one_block, jnp.arange(nblocks, dtype=jnp.int32))
    factor = lax.rsqrt(norm_sum / (MODEL * MOE_FF) + epsilon) / jnp.sqrt(jnp.float32(RANK))
    result = totals * factor[..., None]
    result = result.reshape(nblocks, EXPERTS, TOK_DEV, QUERIES).transpose(1, 0, 2, 3)
    return result.reshape(TOKENS, QUERIES)
```

```python
import functools

import jax
import jax.numpy as jnp
from jax import lax
from jax.experimental import pallas as pl
from jax.experimental.pallas import tpu as pltpu
from jax.sharding import PartitionSpec as P

RANK = 32
TOK_DEV = 256
LANES = 128
PACK = 16
V_PIECES = 2

epsilon = 1e-06
MESH = pl.DeviceIdType.MESH
CONTRACT_LAST = (((1,), (1,)), ((), ()))


def round_up(value, unit):
    return -(-value // unit) * unit


def kernel(
    dims,
    count_ref,
    token_ref,
    acts_hbm,
    grads_hbm,
    gfac_hbm,
    vfac_hbm,
    out_ref,
    acts,
    grads,
    gfac,
    vfac,
    gproj,
    aproj,
    scores,
    onehot,
    dense,
    landed,
    load_sem,
    send_sem,
    recv_sem,
    zsend_sem,
    zrecv_sem,
):
    n_dp, n_exp, across, queries, real_cols = dims
    chips = n_dp // 2
    half = chips // 2
    rows, model = acts.shape
    cols = gfac.shape[2]
    me_e = lax.axis_index("expert")
    me = lax.axis_index("dp")
    core = me % 2
    other = 1 - core

    def walk(index):
        line, at = index // across, index % across
        back = line % 2
        return line * across + at + back * (across - 1 - 2 * at)

    place = walk(me // 2)

    def chip_at(step):
        return walk((place + step + chips) % chips)

    mine = chip_at(0)
    ahead = chip_at(1) * 2 + core
    behind = chip_at(-1) * 2 + core
    partner = mine * 2 + other

    width = model // V_PIECES
    pieces = [None] + [pl.ds(i * width, width) for i in range(V_PIECES)]

    def held(chip, side, piece):
        if pieces[piece] is None:
            return gfac.at[chip, side]
        return vfac.at[chip, side, :, pieces[piece]]

    def own(piece):
        if pieces[piece] is None:
            return gfac_hbm
        return vfac_hbm.at[:, pieces[piece]]

    sent = []

    def send(src, chip, side, piece, target):
        copy = pltpu.make_async_remote_copy(
            src_ref=src,
            dst_ref=held(chip, side, piece),
            send_sem=send_sem.at[len(sent)],
            recv_sem=recv_sem.at[chip, side, piece],
            device_id=(me_e, target),
            device_id_type=MESH,
        )
        copy.start()
        sent.append(copy)

    def arrived(chip, side, piece):
        pltpu.make_async_remote_copy(
            src_ref=held(chip, side, piece),
            dst_ref=held(chip, side, piece),
            send_sem=send_sem.at[0],
            recv_sem=recv_sem.at[chip, side, piece],
            device_id=(me_e, partner),
            device_id_type=MESH,
        ).wait_recv()

    loads = [
        pltpu.make_async_copy(own(j), held(mine, core, j), load_sem.at[j])
        for j in range(len(pieces))
    ]
    load_grads = pltpu.make_async_copy(grads_hbm, grads, load_sem.at[len(pieces)])
    load_acts = pltpu.make_async_copy(acts_hbm, acts, load_sem.at[len(pieces) + 1])

    barrier = pltpu.get_barrier_semaphore()
    for target in (ahead, behind, partner):
        pl.semaphore_signal(barrier, inc=1, device_id=(me_e, target), device_id_type=MESH)
    for i in range(1, n_exp):
        pl.semaphore_signal(
            barrier, inc=1, device_id=((me_e + i) % n_exp, me), device_id_type=MESH
        )
    for copy in loads:
        copy.start()
    load_grads.start()
    load_acts.start()
    pl.semaphore_wait(barrier, 3 + n_exp - 1)

    for j in range(len(pieces)):
        send(own(j), mine, core, j, ahead)
        send(own(j), mine, core, j, behind)
        send(own(j), mine, core, j, partner)

    token_ids = lax.broadcasted_iota(jnp.int32, onehot.shape, 0)
    slot_ids = lax.broadcasted_iota(jnp.int32, (1, rows), 1)
    names = jnp.where(slot_ids < count_ref[0, 0], token_ref[...], -1)
    onehot[...] = (token_ids == names).astype(jnp.float32).astype(onehot.dtype)
    load_grads.wait()
    load_acts.wait()

    def energy(ref):
        total = jnp.zeros((rows, LANES), jnp.float32)
        for i in range(ref.shape[1] // LANES):
            part = ref[:, i * LANES : (i + 1) * LANES].astype(jnp.float32)
            total = total + part * part
        return jnp.sum(total, axis=1, keepdims=True)

    lane_ids = lax.broadcasted_iota(jnp.int32, (rows, LANES), 1)
    scores[...] = jnp.where(lane_ids == queries, energy(acts) * energy(grads), 0.0)

    def project(chip, piece, buf):
        if pieces[piece] is None:
            factor = gfac[chip].reshape(2 * cols, gfac.shape[3])
            gproj[buf] = lax.dot_general(
                grads[...], factor, CONTRACT_LAST, preferred_element_type=jnp.float32
            )
            return
        factor = vfac[chip, :, :, pieces[piece]].reshape(2 * cols, width)
        part = lax.dot_general(
            acts[:, pieces[piece]], factor, CONTRACT_LAST, preferred_element_type=jnp.float32
        )
        if piece == 1:
            aproj[buf] = part
        else:
            aproj[buf] += part

    def score(chip, buf):
        local_ids = lax.broadcasted_iota(jnp.int32, (2 * cols, LANES), 0)
        query_ids = lax.broadcasted_iota(jnp.int32, (2 * cols, LANES), 1)
        second = (local_ids >= cols).astype(jnp.int32)
        column = (2 * chip + second) * real_cols + local_ids - second * cols
        low = query_ids * RANK
        grouping = (column >= low) & (column < low + RANK) & (query_ids < queries)
        grouping = grouping.astype(jnp.float32).astype(jnp.bfloat16)
        product = aproj[buf] * gproj[buf]
        high = product.astype(jnp.bfloat16)
        rest = (product - high.astype(jnp.float32)).astype(jnp.bfloat16)
        scores[...] += jnp.dot(
            high, grouping, preferred_element_type=jnp.float32
        ) + jnp.dot(rest, grouping, preferred_element_type=jnp.float32)

    for j in range(len(pieces)):
        loads[j].wait()
        arrived(mine, other, j)
        project(mine, j, 0)
    score(mine, 0)

    for step in range(1, half + 1):
        last = step == half
        sources = [chip_at(-step)] if last else [chip_at(-step), chip_at(step)]
        for j in range(len(pieces) + 1):
            if j < len(pieces):
                for chip in sources:
                    arrived(chip, core, j)
                    send(held(chip, core, j), chip, core, j, partner)
                if step < half - 1:
                    send(held(sources[0], core, j), sources[0], core, j, ahead)
                    send(held(sources[1], core, j), sources[1], core, j, behind)
                elif step == half - 1:
                    chip = chip_at(step * (2 * core - 1))
                    target = chip_at(1 - 2 * core) * 2 + core
                    send(held(chip, core, j), chip, core, j, target)
            if j > 0:
                for buf, chip in enumerate(sources):
                    arrived(chip, other, j - 1)
                    project(chip, j - 1, buf)
        for buf, chip in enumerate(sources):
            score(chip, buf)

    total = scores[...]
    high = total.astype(jnp.bfloat16)
    rest = (total - high.astype(jnp.float32)).astype(jnp.bfloat16)
    summed = jnp.dot(
        onehot[...],
        jnp.concatenate([high, rest], axis=1),
        preferred_element_type=jnp.float32,
    )
    turned = (summed[:, :LANES] + summed[:, LANES:]).T[: dense.shape[1]]
    for i in range(n_exp):
        dense[i] = turned[:, i * TOK_DEV : (i + 1) * TOK_DEV]
    zcopies = []
    for i in range(1, n_exp):
        target = (me_e + i) % n_exp
        copy = pltpu.make_async_remote_copy(
            src_ref=dense.at[target],
            dst_ref=landed.at[i - 1],
            send_sem=zsend_sem.at[i - 1],
            recv_sem=zrecv_sem.at[i - 1],
            device_id=(target, me),
            device_id_type=MESH,
        )
        copy.start()
        zcopies.append(copy)
    result = dense[me_e]
    for i, copy in enumerate(zcopies):
        copy.wait_recv()
        result = result + landed[i]
    out_ref[...] = result
    for copy in zcopies:
        copy.wait_send()
    for copy in sent:
        copy.wait_send()


def local(dims, row_acts, row_grads, grad_factor, value_factor, counts, row_token):
    n_dp, n_exp, across, queries, real_cols = dims
    gfac, vfac = grad_factor[0].T, value_factor[0].T
    cols = round_up(real_cols, PACK)
    if cols != real_cols:
        pad = ((0, cols - real_cols), (0, 0))
        gfac, vfac = jnp.pad(gfac, pad), jnp.pad(vfac, pad)
    rows, model = row_acts.shape[1:]
    units = row_grads.shape[2]
    chips = n_dp // 2
    depth = round_up(queries + 1, 8)
    n_pieces = 1 + V_PIECES
    bufs = 2
    n_sends = n_pieces * (3 + sum(
        (1 if s == chips // 2 else 3 if s == chips // 2 - 1 else 4)
        for s in range(1, chips // 2 + 1)
    ))
    any_space = pl.BlockSpec(memory_space=pl.ANY)
    sums = pl.pallas_call(
        functools.partial(kernel, dims),
        name="influence_exchange",
        out_shape=jax.ShapeDtypeStruct((depth, TOK_DEV), jnp.float32),
        in_specs=[
            pl.BlockSpec(memory_space=pltpu.SMEM),
            pl.BlockSpec(memory_space=pltpu.VMEM),
            any_space,
            any_space,
            any_space,
            any_space,
        ],
        out_specs=pl.BlockSpec(memory_space=pltpu.VMEM),
        scratch_shapes=[
            pltpu.VMEM((rows, model), jnp.bfloat16),
            pltpu.VMEM((rows, units), jnp.bfloat16),
            pltpu.VMEM((chips, 2, cols, units), jnp.bfloat16),
            pltpu.VMEM((chips, 2, cols, model), jnp.bfloat16),
            pltpu.VMEM((bufs, rows, 2 * cols), jnp.float32),
            pltpu.VMEM((bufs, rows, 2 * cols), jnp.float32),
            pltpu.VMEM((rows, LANES), jnp.float32),
            pltpu.VMEM((n_exp * TOK_DEV, rows), jnp.bfloat16),
            pltpu.VMEM((n_exp, depth, TOK_DEV), jnp.float32),
            pltpu.VMEM((n_exp - 1, depth, TOK_DEV), jnp.float32),
            pltpu.SemaphoreType.DMA((n_pieces + 2,)),
            pltpu.SemaphoreType.DMA((n_sends,)),
            pltpu.SemaphoreType.DMA((chips, 2, n_pieces)),
            pltpu.SemaphoreType.DMA((n_exp - 1,)),
            pltpu.SemaphoreType.DMA((n_exp - 1,)),
        ],
        compiler_params=pltpu.CompilerParams(
            collective_id=0, has_side_effects=True, vmem_limit_bytes=60 * 1024 * 1024
        ),
    )(counts, row_token, row_acts[0], row_grads[0], gfac, vfac)
    factor = lax.rsqrt(sums[queries] / (model * units) + epsilon) / jnp.sqrt(jnp.float32(RANK))
    return (sums[:queries] * factor[None, :]).T


def solution(mesh):
    n_exp, n_dp = mesh.shape["expert"], mesh.shape["dp"]
    across = len({d.coords[0] for d in mesh.devices.flat})

    def whole(row_acts, row_grads, grad_factor, value_factor, counts, row_token):
        all_cols = grad_factor.shape[2]
        dims = (n_dp, n_exp, across, all_cols // RANK, all_cols // n_dp)
        return jax.shard_map(
            functools.partial(local, dims),
            mesh=mesh,
            in_specs=(
                P("expert", "dp", None),
                P("expert", "dp", None),
                P("expert", None, "dp"),
                P("expert", None, "dp"),
                P("expert", "dp"),
                P("expert", "dp"),
            ),
            out_specs=P(("expert", "dp"), None),
            check_vma=False,
        )(row_acts, row_grads, grad_factor, value_factor, counts, row_token)

    return whole
```

```python
import functools

import jax
import jax.numpy as jnp
from jax import lax
from jax.experimental import pallas as pl
from jax.experimental.pallas import tpu as pltpu
from jax.sharding import PartitionSpec as P

RANK = 32
TOK_DEV = 256
LANES = 128
PACK = 16
V_PARTS = (2, 4, 4)

epsilon = 1e-06
MESH = pl.DeviceIdType.MESH
CONTRACT_LAST = (((1,), (1,)), ((), ()))


def round_up(value, unit):
    return -(-value // unit) * unit


def kernel(
    dims,
    count_ref,
    token_ref,
    acts_hbm,
    grads_hbm,
    gfac_hbm,
    vfac_hbm,
    out_ref,
    acts,
    grads,
    gfac,
    vfac,
    gproj,
    aproj,
    scores,
    onehot,
    dense,
    landed,
    far_dense,
    far_landed,
    load_sem,
    send_sem,
    recv_sem,
    zsend_sem,
    zrecv_sem,
):
    n_dp, n_exp, across, queries, real_cols = dims
    chips = n_dp // 2
    half = chips // 2
    rows, model = acts.shape
    cols = gfac.shape[2]
    me_e = lax.axis_index("expert")
    me = lax.axis_index("dp")
    core = me % 2
    other = 1 - core

    def walk(index):
        line, at = index // across, index % across
        back = line % 2
        return line * across + at + back * (across - 1 - 2 * at)

    place = walk(me // 2)

    def chip_at(step):
        return walk((place + step + chips) % chips)

    mine = chip_at(0)
    ahead = chip_at(1) * 2 + core
    behind = chip_at(-1) * 2 + core
    partner = mine * 2 + other

    pieces, start = [None], 0
    for part in V_PARTS:
        pieces.append(pl.ds(start, model // part))
        start += model // part

    def held(chip, side, piece):
        if pieces[piece] is None:
            return gfac.at[chip, side]
        return vfac.at[chip, side, :, pieces[piece]]

    def own(piece):
        if pieces[piece] is None:
            return gfac_hbm
        return vfac_hbm.at[:, pieces[piece]]

    sent = []

    def send(src, chip, side, piece, target):
        copy = pltpu.make_async_remote_copy(
            src_ref=src,
            dst_ref=held(chip, side, piece),
            send_sem=send_sem.at[len(sent)],
            recv_sem=recv_sem.at[chip, side, piece],
            device_id=(me_e, target),
            device_id_type=MESH,
        )
        copy.start()
        sent.append(copy)

    def arrived(chip, side, piece):
        pltpu.make_async_remote_copy(
            src_ref=held(chip, side, piece),
            dst_ref=held(chip, side, piece),
            send_sem=send_sem.at[0],
            recv_sem=recv_sem.at[chip, side, piece],
            device_id=(me_e, partner),
            device_id_type=MESH,
        ).wait_recv()

    loads = [
        pltpu.make_async_copy(own(j), held(mine, core, j), load_sem.at[j])
        for j in range(len(pieces))
    ]
    load_grads = pltpu.make_async_copy(grads_hbm, grads, load_sem.at[len(pieces)])
    load_acts = pltpu.make_async_copy(acts_hbm, acts, load_sem.at[len(pieces) + 1])

    barrier = pltpu.get_barrier_semaphore()
    for target in (ahead, behind, partner):
        pl.semaphore_signal(barrier, inc=1, device_id=(me_e, target), device_id_type=MESH)
    for i in range(1, n_exp):
        pl.semaphore_signal(
            barrier, inc=1, device_id=((me_e + i) % n_exp, me), device_id_type=MESH
        )
    for copy in loads:
        copy.start()
    load_grads.start()
    load_acts.start()
    pl.semaphore_wait(barrier, 3 + n_exp - 1)

    for j in range(len(pieces)):
        send(own(j), mine, core, j, ahead)
        send(own(j), mine, core, j, behind)
        send(own(j), mine, core, j, partner)

    token_ids = lax.broadcasted_iota(jnp.int32, onehot.shape, 0)
    slot_ids = lax.broadcasted_iota(jnp.int32, (1, rows), 1)
    names = jnp.where(slot_ids < count_ref[0, 0], token_ref[...], -1)
    onehot[...] = (token_ids == names).astype(jnp.float32).astype(onehot.dtype)
    load_grads.wait()
    load_acts.wait()

    def energy(ref):
        total = jnp.zeros((rows, LANES), jnp.float32)
        for i in range(ref.shape[1] // LANES):
            part = ref[:, i * LANES : (i + 1) * LANES].astype(jnp.float32)
            total = total + part * part
        return jnp.sum(total, axis=1, keepdims=True)

    lane_ids = lax.broadcasted_iota(jnp.int32, (rows, LANES), 1)
    scores[...] = jnp.where(lane_ids == queries, energy(acts) * energy(grads), 0.0)

    def project_grads(chip, buf):
        factor = gfac[chip].reshape(2 * cols, gfac.shape[3])
        gproj[buf] = lax.dot_general(
            grads[...], factor, CONTRACT_LAST, preferred_element_type=jnp.float32
        )

    def project_acts(chip, span):
        factor = vfac[chip, :, :, span].reshape(2 * cols, span.size)
        return lax.dot_general(
            acts[:, span], factor, CONTRACT_LAST, preferred_element_type=jnp.float32
        )

    def split(value):
        high = value.astype(jnp.bfloat16)
        return high, (value - high.astype(jnp.float32)).astype(jnp.bfloat16)

    def score(chip, product, first):
        local_ids = lax.broadcasted_iota(jnp.int32, (2 * cols, LANES), 0)
        query_ids = lax.broadcasted_iota(jnp.int32, (2 * cols, LANES), 1) + first
        second = (local_ids >= cols).astype(jnp.int32)
        column = (2 * chip + second) * real_cols + local_ids - second * cols
        low = query_ids * RANK
        grouping = (column >= low) & (column < low + RANK) & (query_ids < queries)
        grouping = grouping.astype(jnp.float32).astype(jnp.bfloat16)
        high, rest = split(product)
        return jnp.dot(high, grouping, preferred_element_type=jnp.float32) + jnp.dot(
            rest, grouping, preferred_element_type=jnp.float32
        )

    def hand_over(total, stage, own_sums, others):
        summed = jnp.dot(
            onehot[...],
            jnp.concatenate(split(total), axis=1),
            preferred_element_type=jnp.float32,
        )
        turned = (summed[:, :LANES] + summed[:, LANES:]).T[: own_sums.shape[1]]
        for i in range(n_exp):
            own_sums[i] = turned[:, i * TOK_DEV : (i + 1) * TOK_DEV]
        copies = []
        for i in range(1, n_exp):
            target = (me_e + i) % n_exp
            copy = pltpu.make_async_remote_copy(
                src_ref=own_sums.at[target],
                dst_ref=others.at[i - 1],
                send_sem=zsend_sem.at[stage, i - 1],
                recv_sem=zrecv_sem.at[stage, i - 1],
                device_id=(target, me),
                device_id_type=MESH,
            )
            copy.start()
            copies.append(copy)
        return copies

    def collect(copies, own_sums, others):
        result = own_sums[me_e]
        for i, copy in enumerate(copies):
            copy.wait_recv()
            result = result + others[i]
        return result

    for j in range(len(pieces)):
        loads[j].wait()
        arrived(mine, other, j)
        if j == 0:
            project_grads(mine, 0)
    aproj[0] = project_acts(mine, pl.ds(0, model))
    scores[...] += score(mine, aproj[0] * gproj[0], 0)

    def sources_of(step):
        return [chip_at(-step)] if step == half else [chip_at(-step), chip_at(step)]

    def pass_on(step, j):
        sources = sources_of(step)
        for chip in sources:
            arrived(chip, core, j)
            send(held(chip, core, j), chip, core, j, partner)
        if step < half - 1:
            send(held(sources[0], core, j), sources[0], core, j, ahead)
            send(held(sources[1], core, j), sources[1], core, j, behind)
        elif step == half - 1:
            chip = chip_at(step * (2 * core - 1))
            target = chip_at(1 - 2 * core) * 2 + core
            send(held(chip, core, j), chip, core, j, target)

    far_chip = chip_at(half)
    base = 2 * far_chip * real_cols // RANK

    def multiply(step, j):
        far_scores = None
        for buf, chip in enumerate(sources_of(step)):
            arrived(chip, other, j)
            if j == 0:
                project_grads(chip, buf)
            elif j == 1:
                aproj[buf] = project_acts(chip, pieces[j])
            elif j < len(pieces) - 1:
                aproj[buf] += project_acts(chip, pieces[j])
            else:
                product = (aproj[buf] + project_acts(chip, pieces[j])) * gproj[buf]
                if step == half:
                    far_scores = score(chip, product, base)
                else:
                    scores[...] += score(chip, product, 0)
        return far_scores

    order = [(step, j) for step in range(1, half + 1) for j in range(len(pieces))]
    done, near = 0, None
    for at, (step, j) in enumerate(order):
        pass_on(step, j)
        if step == half and j == 1:
            near = hand_over(scores[...], 0, dense, landed)
        lag = 1 if order[done][0] < half else 2
        if at - done >= lag:
            multiply(*order[done])
            done += 1
    for event in order[done:]:
        far_scores = multiply(*event)

    far = hand_over(far_scores, 1, far_dense, far_landed)
    result = collect(near, dense, landed)
    late = collect(far, far_dense, far_landed)
    row_ids = lax.broadcasted_iota(jnp.int32, result.shape, 0)
    for i in range(late.shape[0]):
        result = result + jnp.where(row_ids == base + i, late[i : i + 1], 0.0)
    energy_sum = result[queries : queries + 1]
    factor = lax.rsqrt(energy_sum / (model * grads.shape[1]) + epsilon)
    factor = factor / jnp.sqrt(jnp.float32(RANK))
    out_ref[...] = result[:queries] * factor
    for copy in near + far + sent:
        copy.wait_send()


def local(dims, row_acts, row_grads, grad_factor, value_factor, counts, row_token):
    n_dp, n_exp, across, queries, real_cols = dims
    gfac, vfac = grad_factor[0].T, value_factor[0].T
    cols = round_up(real_cols, PACK)
    if cols != real_cols:
        pad = ((0, cols - real_cols), (0, 0))
        gfac, vfac = jnp.pad(gfac, pad), jnp.pad(vfac, pad)
    rows, model = row_acts.shape[1:]
    units = row_grads.shape[2]
    chips = n_dp // 2
    depth = round_up(queries + 1, 8)
    n_pieces = 1 + len(V_PARTS)
    few = round_up((2 * real_cols - 1) // RANK + 2, 8)
    bufs = 2
    n_sends = n_pieces * (3 + sum(
        (1 if s == chips // 2 else 3 if s == chips // 2 - 1 else 4)
        for s in range(1, chips // 2 + 1)
    ))
    any_space = pl.BlockSpec(memory_space=pl.ANY)
    turned = pl.pallas_call(
        functools.partial(kernel, dims),
        name="influence_exchange",
        out_shape=jax.ShapeDtypeStruct((queries, TOK_DEV), jnp.float32),
        in_specs=[
            pl.BlockSpec(memory_space=pltpu.SMEM),
            pl.BlockSpec(memory_space=pltpu.VMEM),
            any_space,
            any_space,
            any_space,
            any_space,
        ],
        out_specs=pl.BlockSpec(memory_space=pltpu.VMEM),
        scratch_shapes=[
            pltpu.VMEM((rows, model), jnp.bfloat16),
            pltpu.VMEM((rows, units), jnp.bfloat16),
            pltpu.VMEM((chips, 2, cols, units), jnp.bfloat16),
            pltpu.VMEM((chips, 2, cols, model), jnp.bfloat16),
            pltpu.VMEM((bufs, rows, 2 * cols), jnp.float32),
            pltpu.VMEM((bufs, rows, 2 * cols), jnp.float32),
            pltpu.VMEM((rows, LANES), jnp.float32),
            pltpu.VMEM((n_exp * TOK_DEV, rows), jnp.bfloat16),
            pltpu.VMEM((n_exp, depth, TOK_DEV), jnp.float32),
            pltpu.VMEM((n_exp - 1, depth, TOK_DEV), jnp.float32),
            pltpu.VMEM((n_exp, few, TOK_DEV), jnp.float32),
            pltpu.VMEM((n_exp - 1, few, TOK_DEV), jnp.float32),
            pltpu.SemaphoreType.DMA((n_pieces + 2,)),
            pltpu.SemaphoreType.DMA((n_sends,)),
            pltpu.SemaphoreType.DMA((chips, 2, n_pieces)),
            pltpu.SemaphoreType.DMA((2, n_exp - 1)),
            pltpu.SemaphoreType.DMA((2, n_exp - 1)),
        ],
        compiler_params=pltpu.CompilerParams(
            collective_id=0, has_side_effects=True, vmem_limit_bytes=60 * 1024 * 1024
        ),
    )(counts, row_token, row_acts[0], row_grads[0], gfac, vfac)
    return turned.T


def solution(mesh):
    n_exp, n_dp = mesh.shape["expert"], mesh.shape["dp"]
    across = len({d.coords[0] for d in mesh.devices.flat})

    def whole(row_acts, row_grads, grad_factor, value_factor, counts, row_token):
        all_cols = grad_factor.shape[2]
        dims = (n_dp, n_exp, across, all_cols // RANK, all_cols // n_dp)
        return jax.shard_map(
            functools.partial(local, dims),
            mesh=mesh,
            in_specs=(
                P("expert", "dp", None),
                P("expert", "dp", None),
                P("expert", None, "dp"),
                P("expert", None, "dp"),
                P("expert", "dp"),
                P("expert", "dp"),
            ),
            out_specs=P(("expert", "dp"), None),
            check_vma=False,
        )(row_acts, row_grads, grad_factor, value_factor, counts, row_token)

    return whole
```
